256 devices in a mesh: copy: 2 (over y_hi), dp: 8 (over x, core), fsdp: 16 (over y_lo, z).
Axes of the slice: x: 4, y: 4 (y_hi: 2, y_lo: 2; y = y_hi * 2 + y_lo), z: 8, core: 2. Of those that a mesh axis runs over, the one named last changes fastest.
Arguments:
- queries: bfloat16 [2, 128, 256, 2560], P('copy', ('dp', 'fsdp')), may hold values from -25 to 25
- keys: bfloat16 [2, 128, 256, 2560], P('copy', ('dp', 'fsdp')), may hold values from -25 to 25
- values: bfloat16 [2, 128, 256, 2560], P('copy', ('dp', 'fsdp')), may hold values from -6 to 6
- residual: bfloat16 [2, 128, 256, 2560], P('copy', ('dp', 'fsdp')), may hold values from -6 to 6
- event_ids: int32 [128, 256], P(('dp', 'fsdp')), may hold values from 0 to 1023
- lengths: int32 [128], replicated, may hold values from 8 to 256, as said below
- type_weight: float32 [1024], replicated, may hold values from 0.25 to 4
- w_out: bfloat16 [2, 2560, 2560], P('copy', 'fsdp'), may hold values from -0.125 to 0.125
- gain: float32 [2, 2560], P('copy'), may hold values from 0.5 to 1.5
Outputs:
- loss: float32 [2, 128], P('copy', ('dp', 'fsdp'))
- d_queries: bfloat16 [2, 128, 256, 2560], P('copy', ('dp', 'fsdp'))
- d_keys: bfloat16 [2, 128, 256, 2560], P('copy', ('dp', 'fsdp'))
- d_values: bfloat16 [2, 128, 256, 2560], P('copy', ('dp', 'fsdp'))
- d_wo: float32 [2, 2560, 2560], P('copy', 'fsdp')
The draws below stay inside these ranges and needn't reach their ends.
Inputs may be any that keep to these rules, and one draw needn't show every extreme that they name: `lengths`: every history has at least 8 valid events and some history has all 256.
All inputs are finite; a program needn't handle non-finite values.
Results may differ from the reference program's by a relative error of at most 0.02.
Values may be sent and summed in bfloat16 or wider, within the bound.
A program may use at most 128 MiB of HBM per device.

```python
import math
import jax
import jax.numpy as jnp
import numpy as np
from jax import lax

D = 2560
H = 20
DH = 128
L = 256
TYPES = 1024
HD = 2560
HISTS = 128


def drawn_pair(key):
    query_key = jax.random.fold_in(key, 11)
    key_key = jax.random.fold_in(key, 12)
    shape = (2, HISTS, L, H, DH)
    query_draw = jnp.clip(jax.random.normal(query_key, shape, jnp.float32), -6.0, 6.0)
    key_draw = jnp.clip(jax.random.normal(key_key, shape, jnp.float32), -6.0, 6.0)
    return (query_draw.reshape(2, HISTS, L, HD), key_draw.reshape(2, HISTS, L, HD))


def draw_queries(key, part):
    return drawn_pair(key)[0].astype(jnp.bfloat16)


def draw_keys(key, part):
    return drawn_pair(key)[1].astype(jnp.bfloat16)


def draw_lengths(key, part):
    drawn = jax.random.randint(jax.random.fold_in(key, 21), (HISTS,), 8, L + 1, dtype=jnp.int32)
    return drawn.at[0].set(L)


def set_ends(values, stream_key, smallest, largest):
    spot = [jax.random.randint(jax.random.fold_in(stream_key, axis), (), 0, length) for axis, length in enumerate(values.shape)]
    longest = values.shape.index(max(values.shape))
    next_to = spot[:longest] + [(spot[longest] + 1) % values.shape[longest]] + spot[longest + 1:]
    return values.at[tuple(spot)].set(smallest).at[tuple(next_to)].set(largest)


def block_levels(stream_key, dims, split, low, largest):
    def one(axis_at, blocks):
        steps = jax.random.uniform(jax.random.fold_in(jax.random.fold_in(stream_key, 6), axis_at), (blocks,), jnp.float32, low / len(split), largest / len(split))
        return jnp.repeat(jnp.exp(steps), dims[axis_at] // blocks).reshape((-1,) + (1,) * (len(dims) - axis_at - 1))

    level = one(*split[0])
    for cut in split[1:]:
        level = level * one(*cut)
    return level


def rank_bounds(amount, skew):
    portions = [(1 << 20) // math.isqrt(standing ** skew) + 1 for standing in range(1, amount + 1)]
    scale = 1 + sum(portions) // (1 << 30)
    return np.cumsum(np.array([max(1, weight // scale) for weight in portions]))


def ranked(stream_key, extent, number_of, lean):
    listing = rank_bounds(number_of, lean)
    ticket = jax.random.randint(jax.random.fold_in(stream_key, 1), extent, 0, int(listing[number_of - 1]))
    rank = jnp.searchsorted(jnp.asarray(listing, jnp.int32), ticket, side="right")
    return jax.random.permutation(jax.random.fold_in(stream_key, 2), number_of)[rank].astype(jnp.int32)


def bell_draw(own_key, shape, deviation, limit, pieces=(), kind=jnp.bfloat16):
    result = deviation * jax.random.normal(own_key, shape, jnp.float32)
    if pieces:
        result = result * block_levels(own_key, shape, pieces, -0.22, 0.18)
    return jnp.clip(result, -limit, limit).astype(kind)


def setup_inputs(seed: int = 0) -> dict:
    arg_keys = jax.random.split(jax.random.key(seed), 10)
    return {
        "queries": draw_queries(jax.random.fold_in(arg_keys[9], 71), 0),
        "keys": draw_keys(jax.random.fold_in(arg_keys[9], 71), 0),
        "values": bell_draw(arg_keys[2], (2, HISTS, L, HD), 1.0, 6.0, ((0, 2), (1, 128))),
        "residual": bell_draw(arg_keys[3], (2, HISTS, L, D), 1.0, 6.0, ((0, 2), (1, 128))),
        "event_ids": set_ends(ranked(arg_keys[4], (HISTS, L), TYPES, 2), jax.random.fold_in(arg_keys[4], 3), 0, TYPES - 1).astype(jnp.int32),
        "lengths": draw_lengths(jax.random.fold_in(arg_keys[9], 71), 0),
        "type_weight": jnp.clip(jnp.exp(jax.random.uniform(arg_keys[6], (TYPES,), jnp.float32, math.log(0.25), math.log(4.0))), 0.25, 4.0),
        "w_out": bell_draw(arg_keys[7], (2, HD, D), HD ** -0.5, 0.125, ((0, 2), (1, 16))),
        "gain": jnp.clip(1.0 + 0.1 * jax.random.normal(arg_keys[8], (2, D), jnp.float32), 0.5, 1.5),
    }


def attention_forward(queries, keys, values, residual, w_out, gain, length):
    query_heads = queries.reshape(L, H, DH).astype(jnp.float32)
    key_heads = keys.reshape(L, H, DH).astype(jnp.float32)
    value_heads = values.reshape(L, H, DH).astype(jnp.float32)
    scores = jnp.einsum('qhd,khd->hqk', query_heads, key_heads) / jnp.sqrt(jnp.float32(DH))
    rows = jnp.arange(L, dtype=jnp.int32)[:, None]
    cols = jnp.arange(L, dtype=jnp.int32)[None, :]
    valid = (cols <= rows) & (cols < length)
    scores = jnp.where(valid[None], scores, jnp.float32(-1e+30))
    probs = jax.nn.softmax(scores, axis=-1)
    probs_b = probs.astype(jnp.bfloat16)
    attn = jnp.einsum('hqk,khd->qhd', probs_b.astype(jnp.float32), value_heads).reshape(L, HD).astype(jnp.bfloat16)
    hidden = residual.astype(jnp.float32) + jnp.dot(attn, w_out, preferred_element_type=jnp.float32)
    inv = lax.rsqrt(lax.optimization_barrier(jnp.mean(hidden * hidden, axis=-1, keepdims=True)) + 1e-06)
    normed = hidden * inv
    feat = normed * gain[None, :]
    return (probs, probs_b, attn, inv, normed, feat)

def attention_backward(queries, keys, values, w_out, gain, probs, probs_b, attn, inv, normed, feat, partner, tok_w, count):
    diff = feat - partner.astype(jnp.float32)
    loss = jnp.sum(tok_w * lax.optimization_barrier(jnp.sum(diff * diff, axis=-1))) / (D * count)
    dfeat = 2.0 * tok_w[:, None] * diff / (D * count)
    scaled = dfeat * gain[None, :]
    d_hidden = (inv * (scaled - normed * lax.optimization_barrier(jnp.mean(normed * scaled, axis=-1, keepdims=True)))).astype(jnp.bfloat16)
    partial_value = jnp.dot(attn.T, d_hidden, preferred_element_type=jnp.float32).astype(jnp.bfloat16).astype(jnp.float32)
    d_attn = jnp.dot(d_hidden, w_out.T, preferred_element_type=jnp.float32).astype(jnp.bfloat16)
    d_heads = d_attn.reshape(L, H, DH).astype(jnp.float32)
    query_heads = queries.reshape(L, H, DH).astype(jnp.float32)
    key_heads = keys.reshape(L, H, DH).astype(jnp.float32)
    value_heads = values.reshape(L, H, DH).astype(jnp.float32)
    d_values = jnp.einsum('hqk,qhd->khd', probs_b.astype(jnp.float32), d_heads).reshape(L, HD).astype(jnp.bfloat16)
    dprob = jnp.einsum('qhd,khd->hqk', d_heads, value_heads)
    delta = lax.optimization_barrier(jnp.sum(dprob * probs, axis=-1, keepdims=True))
    ds = (probs * (dprob - delta) / jnp.sqrt(jnp.float32(DH))).astype(jnp.bfloat16).astype(jnp.float32)
    d_queries = jnp.einsum('hqk,khd->qhd', ds, key_heads).reshape(L, HD).astype(jnp.bfloat16)
    d_keys = jnp.einsum('hqk,qhd->khd', ds, query_heads).reshape(L, HD).astype(jnp.bfloat16)
    return (loss, d_queries, d_keys, d_values, partial_value)

def reference(queries, keys, values, residual, event_ids, lengths, type_weight, w_out, gain):
    count = jnp.sum(lengths).astype(jnp.float32)
    forward = jax.vmap(attention_forward, in_axes=(0, 0, 0, 0, 0, 0, None))
    backward = jax.vmap(attention_backward, in_axes=(0, 0, 0, 0, 0, 0, 0, 0, 0, 0, 0, 0, None, None))

    def one_history(carry, index):
        q_hist = queries[:, index]
        k_hist = keys[:, index]
        v_hist = values[:, index]
        x_hist = residual[:, index]
        length = lengths[index]
        probs, probs_b, attn, inv, normed, feat = forward(q_hist, k_hist, v_hist, x_hist, w_out, gain, length)
        partner = feat.astype(jnp.bfloat16)[::-1]
        live = jnp.arange(L, dtype=jnp.int32) < length
        tok_w = jnp.where(live, type_weight[event_ids[index]], jnp.float32(0.0))
        loss, d_q, d_k, d_v, partial_value = backward(q_hist, k_hist, v_hist, w_out, gain, probs, probs_b, attn, inv, normed, feat, partner, tok_w, count)
        return (carry + partial_value, (loss, d_q, d_k, d_v))
    start = jnp.zeros((2, HD, D), jnp.float32)
    d_wo, (loss, d_q, d_k, d_v) = lax.scan(one_history, start, jnp.arange(HISTS, dtype=jnp.int32))
    return (jnp.transpose(loss, (1, 0)), jnp.transpose(d_q, (1, 0, 2, 3)), jnp.transpose(d_k, (1, 0, 2, 3)), jnp.transpose(d_v, (1, 0, 2, 3)), d_wo)
```

```python
import jax
import jax.numpy as jnp
from jax import lax
from jax.experimental import pallas as pl
from jax.experimental.pallas import tpu as pltpu
from jax.sharding import PartitionSpec as P

MESH = pl.DeviceIdType.MESH
F32 = jnp.float32
BF16 = jnp.bfloat16
L, D, H, DH = 256, 2560, 20, 128
BLK = 160
HALF = 80
QW = 640
CW = 1280
AW, BW = 256, 384
SCALE = 128.0**0.5
NT = (((1,), (1,)), ((), ()))
TN = (((0,), (0,)), ((), ()))
NEAR = (0, -1, 1, -2, 2, -3, 3, -4)


def dot(a, b, dims=(((1,), (0,)), ((), ()))):
    return lax.dot_general(a, b, dims, preferred_element_type=F32)


def kernel(
    q_ref, k_ref, v_ref, res_ref, w_ref, ids_ref, len_ref, tw_ref, gain_ref,
    loss_ref, dq_ref, dk_ref, dv_ref, dwo_ref,
    wf, at, hid, pb, gp, dh, dhs, probs, bias, pbuf, za, zaf, xa, xb, zb, fsum, yrx, rows,
    s_send, s_zr, s_xr, s_yr, s_sib, s_pr, s_misc, s_za, s_xa, s_xb, s_zb, s_fin,
):
    attn, hb = dk_ref, dq_ref
    c = lax.axis_index("copy")
    d = lax.axis_index("dp")
    f = lax.axis_index("fsdp")
    x, core = d // 2, d % 2
    y, z = f // 8, f % 8
    own = d * 16 + f

    def at_z(step):
        return (c, d, y * 8 + (z + step + 8) % 8)

    def at_x(step):
        return (c, ((x + step + 4) % 4) * 2 + core, f)

    other_y = (c, d, (1 - y) * 8 + z)
    sibling = (c, x * 2 + 1 - core, f)
    partner = (1 - c, d, f)

    def send(src, dst, group, recv, device):
        copy = pltpu.make_async_remote_copy(
            src_ref=src, dst_ref=dst, send_sem=s_send.at[group], recv_sem=recv,
            device_id=device, device_id_type=MESH,
        )
        copy.start()

    def arrived(ref, sem):
        pltpu.make_async_copy(ref, ref, sem).wait()

    barrier = pltpu.get_barrier_semaphore()
    greet = (at_z(1), at_z(-1), at_x(1), at_x(-1), at_x(2), other_y, sibling, partner)
    for device in greet:
        pl.semaphore_signal(barrier, inc=1, device_id=device, device_id_type=MESH)
    pl.semaphore_wait(barrier, len(greet))

    def piece(yy, zz, quarter):
        row = pl.multiple_of((yy * 8 + (zz + 16) % 8) * BLK + core * HALF, 16)
        col = pl.multiple_of(((quarter + 8) % 4) * QW, 128)
        return wf.at[pl.ds(row, HALF), pl.ds(col, QW)]

    def own_piece(quarter):
        col = pl.multiple_of(((quarter + 8) % 4) * QW, 128)
        return w_ref.at[pl.ds(pl.multiple_of(core * HALF, 16), HALF), pl.ds(col, QW)]

    ORDER = (0, 1, -1, 2)

    def steps(s, way):
        return 4 if (s + way) % 2 == 0 else 3

    def z_where(s):
        return ((1 - y), x) if s == 0 else (y, x + ORDER[s - 1])

    def to_sibling(ref, i):
        send(ref, ref, 0, s_sib.at[i], sibling)

    def z_event(s, k):
        yy, quarter = z_where(s)
        i = 0 if s == 0 else s - 1
        for way, sign in ((0, 1), (1, -1)):
            last = steps(s, way)
            if 0 < k <= last:
                got = piece(yy, z - sign * k, quarter)
                arrived(got, s_zr.at[s, way, k - 1])
                if k < last:
                    send(got, got, 0, s_zr.at[s, way, k], at_z(sign))
                if s == 0:
                    x_send(NEAR.index(-sign * k) if k < 4 else 7)
                to_sibling(got, i)
            elif k == 0:
                dst = piece(yy, z, quarter)
                src = dst if s == 0 else own_piece(quarter)
                send(src, dst, 0, s_zr.at[s, way, 0], at_z(sign))

    def x_send(m):
        got = piece(1 - y, z + NEAR[m], x)
        send(got, got, 0, s_xr.at[0, m], at_x(1))
        send(got, got, 0, s_xr.at[1, m], at_x(-1))

    def x_event(m):
        for way, sign in ((0, 1), (1, -1)):
            got = piece(1 - y, z + NEAR[m], x - sign)
            arrived(got, s_xr.at[way, m])
            if m % 2 == way:
                send(got, got, 0, s_xr.at[way, 8 + m // 2], at_x(sign))
            to_sibling(got, 1 if way == 1 else 2)

    def x_last(n):
        for way in (0, 1):
            got = piece(1 - y, z + NEAR[2 * n + way], x + 2)
            arrived(got, s_xr.at[way, 8 + n])
            to_sibling(got, 3)

    src = own_piece(x)
    send(src, piece(y, z, x), 0, s_yr.at[0], other_y)
    z_event(1, 0)
    z_event(2, 0)
    send(gain_ref, gp, 1, s_misc.at[0], partner)
    local = pltpu.make_async_copy(
        w_ref, wf.at[pl.ds(pl.multiple_of(f * BLK, 16), BLK), :], s_misc.at[2]
    )
    local.start()

    lane = lax.broadcasted_iota(jnp.int32, (1, 128), 1)
    lens = len_ref[...]
    count = jnp.sum(lens).astype(F32)
    length = jnp.sum(jnp.where(lane == own, lens, 0), axis=-1, keepdims=True)
    r_at = lax.broadcasted_iota(jnp.int32, (L, L), 0)
    c_at = lax.broadcasted_iota(jnp.int32, (L, L), 1)
    bias[...] = jnp.where((c_at <= r_at) & (c_at < length), F32(0.0), F32(-1e30))

    def head(h):
        return pl.ds(pl.multiple_of(h * DH, DH), DH)

    def forward(h, carry):
        cols = head(h)
        s = dot(q_ref[:, cols], k_ref[:, cols], NT) * F32(1.0 / SCALE) + bias[...]
        e = jnp.exp(s - jnp.max(s, axis=-1, keepdims=True))
        p = (e / jnp.sum(e, axis=-1, keepdims=True)).astype(BF16)
        probs[h] = p
        a = dot(p, v_ref[:, cols])
        attn[:, cols] = a.astype(BF16)
        at[cols, 0:L] = a.T.astype(BF16)
        return carry

    def heads(first, n):
        lax.fori_loop(first, first + n, forward, 0)

    heads(0, 2)
    got = piece(1 - y, z, x)
    arrived(got, s_yr.at[0])
    z_event(0, 0)
    x_send(0)
    to_sibling(got, 0)
    heads(2, 3)
    z_event(1, 1)
    z_event(0, 1)
    heads(5, 3)
    z_event(1, 2)
    z_event(0, 2)
    x_event(0)
    heads(8, 4)
    z_event(1, 3)
    z_event(0, 3)
    x_event(1)
    x_event(2)
    heads(12, 4)
    z_event(1, 4)
    z_event(0, 4)
    z_event(2, 1)
    z_event(3, 0)
    x_event(3)
    x_event(4)
    heads(16, 4)
    send(at.at[:, 0:L], at.at[:, L : 2 * L], 1, s_misc.at[1], sibling)
    z_event(2, 2)
    z_event(3, 1)
    z_event(4, 0)
    x_event(5)
    x_event(6)

    type_at = lax.broadcasted_iota(jnp.int32, (1, 1024), 1)
    looked = jnp.sum(
        jnp.where(ids_ref[...] == type_at, tw_ref[...], F32(0.0)), axis=-1, keepdims=True
    )
    live = lax.broadcasted_iota(jnp.int32, (L, 1), 0) < length
    rows[:, 0:1] = jnp.where(live, looked, F32(0.0))
    rows[:, 1:2] = jnp.zeros((L, 1), F32)
    rows[:, 2:3] = jnp.zeros((L, 1), F32)
    local.wait()

    def quarter_cols(i):
        return pl.ds(pl.multiple_of(((x + ORDER[i] + 4) % 4) * QW, 128), QW)

    def hidden(i):
        arrived(wf.at[0 : 15 * HALF, 0:QW], s_sib.at[i])
        cols = quarter_cols(i)
        hc = res_ref[:, cols].astype(F32) + dot(attn[...], wf[:, cols])
        hid[:, cols] = hc
        hb[:, cols] = hc.astype(BF16)
        rows[:, 1:2] += jnp.sum(hc * hc, axis=-1, keepdims=True)
        send(hb.at[:, cols], pb.at[:, cols], 2, s_pr.at[i], partner)

    def partner_square(i):
        cols = quarter_cols(i)
        arrived(pb.at[:, cols], s_pr.at[i])
        part = pb[:, cols].astype(F32)
        rows[:, 2:3] += jnp.sum(part * part, axis=-1, keepdims=True)

    hidden(0)
    z_event(2, 3)
    z_event(3, 2)
    z_event(4, 1)
    x_event(7)
    z_event(2, 4)
    hidden(1)
    z_event(3, 3)
    z_event(4, 2)
    for n in range(4):
        x_last(n)
    z_event(3, 4)
    hidden(2)
    z_event(4, 3)
    z_event(4, 4)
    hidden(3)
    arrived(gp, s_misc.at[0])
    arrived(at.at[:, L : 2 * L], s_misc.at[1])
    for i in range(4):
        partner_square(i)

    tok = rows[:, 0:1]
    inv = lax.rsqrt(rows[:, 1:2] * F32(1.0 / D) + F32(1e-06))
    inv_p = lax.rsqrt(rows[:, 2:3] * F32(1.0 / D) + F32(1e-06))
    coef = 2.0 * tok / (D * count)
    rows[:, 3:4] = jnp.zeros((L, 1), F32)
    rows[:, 4:5] = jnp.zeros((L, 1), F32)

    def chunk(t):
        return pl.ds(pl.multiple_of(t * 256, 256), 256)

    def stats(t, carry):
        cols = chunk(t)
        n = hid[:, cols] * inv
        g = gain_ref[:, cols]
        diff = n * g - pb[:, cols].astype(F32) * inv_p * gp[:, cols]
        scaled = diff * g
        rows[:, 3:4] += jnp.sum(diff * diff, axis=-1, keepdims=True)
        rows[:, 4:5] += jnp.sum(n * scaled, axis=-1, keepdims=True)
        return carry

    lax.fori_loop(0, 10, stats, 0)
    loss_ref[...] = jnp.sum(tok * rows[:, 3:4], axis=0, keepdims=True) / (D * count)
    mean = rows[:, 4:5] * F32(1.0 / D)

    def grads(t, carry):
        cols = chunk(t)
        n = hid[:, cols] * inv
        g = gain_ref[:, cols]
        diff = n * g - pb[:, cols].astype(F32) * inv_p * gp[:, cols]
        dh[:, cols] = (inv * coef * (diff * g - n * mean)).astype(BF16)
        return carry

    lax.fori_loop(0, 10, grads, 0)
    other_half = pl.ds(pl.multiple_of((1 - core) * CW, 128), CW)
    send(dh.at[:, other_half], dhs, 1, s_misc.at[3], sibling)
    arrived(dhs, s_misc.at[3])

    def term(row, n_rows, col, width):
        r = pl.ds(pl.multiple_of(row, 16), n_rows)
        mine = dh[:, pl.ds(pl.multiple_of(core * CW + col, 128), width)]
        return dot(at[r, 0:L], mine) + dot(at[r, L : 2 * L], dhs[:, col : col + width])

    def block_row(yy, zz):
        return (yy * 8 + (zz + 16) % 8) * BLK

    WAYS = ((0, 1), (1, -1))

    def b_first(t):
        for way, sign in WAYS:
            for yy in (0, 1):
                val = term(block_row(yy, z - sign * (1 + t)), BLK, 2 * AW + way * BW, BW)
                pbuf[way, t, :, yy] = val.reshape(4, 40, BW).astype(BF16)
            send(
                pbuf.at[way, t, (x - sign + 4) % 4], xb.at[way, 0, t], 4,
                s_xb.at[way, 0, t], at_x(sign),
            )

    def b_next(t, k):
        for way, sign in WAYS:
            slot = xb.at[way, k - 1, t]
            arrived(slot, s_xb.at[way, k - 1, t])
            mine = pbuf[way, t, (x - sign * (1 + k) + 8) % 4]
            slot[...] = (slot[...].astype(F32) + mine.astype(F32)).astype(BF16)
            send(slot, xb.at[way, k, t], 4, s_xb.at[way, k, t], at_x(sign))

    def b_sum(way, t):
        slot = xb.at[way, 2, t]
        arrived(slot, s_xb.at[way, 2, t])
        return slot[...].astype(F32) + pbuf[way, t, x].astype(F32)

    def b_z(t):
        for way, sign in WAYS:
            val = b_sum(way, t)
            slot = zb.at[way, t]

            @pl.when(t == 0)
            def _():
                slot[...] = val.astype(BF16)

            @pl.when(t > 0)
            def _():
                arrived(slot, s_zb.at[way, t])
                slot[...] = (slot[...].astype(F32) + val).astype(BF16)

            send(slot, zb.at[way, t + 1], 5, s_zb.at[way, t + 1], at_z(sign))

    def a_step(t):
        for yy in (0, 1):
            for way, sign in WAYS:
                val = term(block_row(yy, z - sign * (1 + t)), BLK, way * AW, AW)
                slot = za.at[way, yy, t]

                @pl.when(t == 0)
                def _():
                    slot[...] = val.astype(BF16)

                @pl.when(t > 0)
                def _():
                    arrived(slot, s_za.at[way, yy, t])
                    slot[...] = (slot[...].astype(F32) + val).astype(BF16)

                send(slot, za.at[way, yy, t + 1], 3, s_za.at[way, yy, t + 1], at_z(sign))

    def a_last():
        for way, sign in WAYS:
            for yy in (0, 1):
                slot = za.at[way, yy, 7]
                arrived(slot, s_za.at[way, yy, 7])
                val = slot[...].astype(F32) + term(block_row(yy, z), BLK, way * AW, AW)
                zaf[way, :, yy] = val.reshape(4, 40, AW).astype(BF16)
            send(zaf.at[way, (x - sign + 4) % 4], xa.at[way, 0], 6, s_xa.at[way, 0], at_x(sign))

    def a_next(k):
        for way, sign in WAYS:
            slot = xa.at[way, k - 1]
            arrived(slot, s_xa.at[way, k - 1])
            mine = zaf[way, (x - sign * (1 + k) + 8) % 4]
            slot[...] = (slot[...].astype(F32) + mine.astype(F32)).astype(BF16)
            send(slot, xa.at[way, k], 6, s_xa.at[way, k], at_x(sign))

    def pair(t):
        cols2 = pl.ds(pl.multiple_of(t * 256, 256), 256)
        da2 = dot(dh[...], wf[cols2, :], NT).astype(BF16)
        for j in (0, 1):
            cols = pl.ds(pl.multiple_of(t * 256 + j * DH, DH), DH)
            da = da2[:, j * DH : (j + 1) * DH]
            p = probs[2 * t + j]
            dv_ref[:, cols] = dot(p, da, TN).astype(BF16)
            dprob = dot(da, v_ref[:, cols], NT)
            pf = p.astype(F32)
            delta = jnp.sum(dprob * pf, axis=-1, keepdims=True)
            ds = (pf * (dprob - delta) * F32(1.0 / SCALE)).astype(BF16)
            dq_ref[:, cols] = dot(ds, k_ref[:, cols]).astype(BF16)
            dk_ref[:, cols] = dot(ds, q_ref[:, cols], TN).astype(BF16)

    arrived(pb, s_send.at[2])

    def tick(t, carry):
        @pl.when(t < 8)
        def _():
            b_first(t)

        @pl.when(t < 7)
        def _():
            a_step(t)

        @pl.when((t >= 1) & (t < 9))
        def _():
            b_next(t - 1, 1)

        @pl.when((t >= 2) & (t < 10))
        def _():
            b_next(t - 2, 2)

        @pl.when((t >= 3) & (t < 10))
        def _():
            b_z(t - 3)

        @pl.when(t == 7)
        def _():
            a_last()

        @pl.when(t == 8)
        def _():
            a_next(1)

        @pl.when(t == 9)
        def _():
            a_next(2)

        pair(t)
        return carry

    lax.fori_loop(0, 10, tick, 0)

    for way, sign in WAYS:
        slot = xa.at[way, 2]
        arrived(slot, s_xa.at[way, 2])
        val = slot[...].astype(F32) + zaf[way, x].astype(F32)
        fsum[:, :, way * AW : (way + 1) * AW] = val.astype(BF16)
    for way, sign in WAYS:
        val = b_sum(way, 7)
        slot = zb.at[way, 7]
        arrived(slot, s_zb.at[way, 7])
        lo = 2 * AW + way * BW
        fsum[:, :, lo : lo + BW] = (slot[...].astype(F32) + val).astype(BF16)
    send(fsum.at[1 - y], yrx, 7, s_fin.at[0], other_y)
    half = pl.ds(pl.multiple_of(core * CW, 128), CW)
    arrived(yrx, s_fin.at[0])
    dwo_ref[x, :, half] = (yrx[...].astype(F32) + fsum[y].astype(F32)).astype(BF16)
    mine = dwo_ref.at[x, :, half]
    for i, step in enumerate((1, -1, 2)):
        send(mine, mine, 7, s_fin.at[1 + i], at_x(step))
    send(mine, mine, 7, s_fin.at[4], sibling)
    for i, step in enumerate((1, -1, 2)):
        got = dwo_ref.at[(x - step + 4) % 4, :, half]
        arrived(got, s_fin.at[1 + i])
        send(got, got, 7, s_fin.at[5 + i], sibling)
    for i, step in enumerate((0, 1, -1, 2)):
        got = dwo_ref.at[(x - step + 4) % 4, :, other_half]
        arrived(got, s_fin.at[4 + i])

    arrived(wf.at[0 : 32 * HALF, 0:QW], s_send.at[0])
    arrived(wf.at[0 : 32 * HALF, 0:QW], s_send.at[0])
    arrived(wf.at[0 : 32 * HALF, 0:QW], s_send.at[0])
    arrived(wf.at[0 : 24 * HALF, 0:QW], s_send.at[0])
    arrived(gp, s_send.at[1])
    arrived(at.at[:, 0:L], s_send.at[1])
    arrived(dhs, s_send.at[1])
    for way in (0, 1):
        for yy in (0, 1):
            arrived(za.at[way, yy, 1:8], s_send.at[3])
        arrived(xb.at[way], s_send.at[4])
        arrived(zb.at[way, 1:8], s_send.at[5])
        arrived(xa.at[way], s_send.at[6])
    arrived(yrx, s_send.at[7])
    for _ in range(7):
        arrived(yrx, s_send.at[7])


def body(queries, keys, values, residual, event_ids, lengths, type_weight, w_out, gain):
    vmem = pl.BlockSpec(memory_space=pltpu.VMEM)
    dma = pltpu.SemaphoreType.DMA
    big = jax.ShapeDtypeStruct((L, D), BF16)
    loss, dq, dk, dv, dwo = pl.pallas_call(
        kernel,
        out_shape=(
            jax.ShapeDtypeStruct((1, 1), F32), big, big, big,
            jax.ShapeDtypeStruct((4, 40, D), BF16),
        ),
        in_specs=[vmem] * 9,
        out_specs=(vmem,) * 5,
        scratch_shapes=[
            pltpu.VMEM((D, D), BF16),
            pltpu.VMEM((D, 2 * L), BF16),
            pltpu.VMEM((L, D), F32),
            pltpu.VMEM((L, D), BF16),
            pltpu.VMEM((1, D), F32),
            pltpu.VMEM((L, D), BF16),
            pltpu.VMEM((L, CW), BF16),
            pltpu.VMEM((H, L, L), BF16),
            pltpu.VMEM((L, L), F32),
            pltpu.VMEM((2, 8, 4, 2, 40, BW), BF16),
            pltpu.VMEM((2, 2, 8, BLK, AW), BF16),
            pltpu.VMEM((2, 4, 2, 40, AW), BF16),
            pltpu.VMEM((2, 3, 2, 40, AW), BF16),
            pltpu.VMEM((2, 3, 8, 2, 40, BW), BF16),
            pltpu.VMEM((2, 8, 2, 40, BW), BF16),
            pltpu.VMEM((2, 40, CW), BF16),
            pltpu.VMEM((40, CW), BF16),
            pltpu.VMEM((L, 128), F32),
            dma((8,)),
            dma((5, 2, 4)),
            dma((2, 12)),
            dma((1,)),
            dma((4,)),
            dma((4,)),
            dma((4,)),
            dma((2, 2, 8)),
            dma((2, 3)),
            dma((2, 3, 8)),
            dma((2, 8)),
            dma((8,)),
        ],
        compiler_params=pltpu.CompilerParams(
            collective_id=0, has_side_effects=True, vmem_limit_bytes=67043328
        ),
        name="step",
    )(
        queries[0, 0], keys[0, 0], values[0, 0], residual[0, 0], w_out[0],
        event_ids.reshape(L, 1), lengths.reshape(1, 128), type_weight.reshape(1, 1024), gain,
    )
    return (
        loss, dq[None, None], dk[None, None], dv[None, None],
        dwo.reshape(BLK, D).astype(F32)[None],
    )


def solution(mesh):
    hist = P("copy", ("dp", "fsdp"), None, None)
    return jax.shard_map(
        body,
        mesh=mesh,
        in_specs=(
            hist, hist, hist, hist, P(("dp", "fsdp"), None), P(), P(),
            P("copy", "fsdp", None), P("copy", None),
        ),
        out_specs=(
            P("copy", ("dp", "fsdp")), hist, hist, hist, P("copy", "fsdp", None),
        ),
        check_vma=False,
    )
```

```python
import jax
import jax.numpy as jnp
from jax import lax
from jax.experimental import pallas as pl
from jax.experimental.pallas import tpu as pltpu
from jax.sharding import PartitionSpec as P

MESH = pl.DeviceIdType.MESH
F32 = jnp.float32
BF16 = jnp.bfloat16
L, D, H, DH = 256, 2560, 20, 128
BLK = 160
HALF = 80
QW = 640
CW = 1280
AW, BW = 256, 384
SCALE = 128.0**0.5
NT = (((1,), (1,)), ((), ()))
TN = (((0,), (0,)), ((), ()))
NEAR = (0, -1, 1, -2, 2, -3, 3, -4)


def dot(a, b, dims=(((1,), (0,)), ((), ()))):
    return lax.dot_general(a, b, dims, preferred_element_type=F32)


def kernel(
    q_hbm, k_hbm, v_hbm, res_hbm, w_ref, ids_ref, len_ref, tw_ref, gain_ref,
    loss_ref, dq_ref, dk_ref, dv_ref, dwo_ref,
    q_ref, k_ref, v_ref, res_ref, wf, at, hid, pb, gp, dh, dhs, probs, bias, pbuf, za, zaf, xa, xb, zb, fsum, yrx, rows, dab, ivs, ivr, acc,
    s_send, s_zr, s_xr, s_yr, s_sib, s_pr, s_misc, s_za, s_xa, s_xb, s_zb, s_fin, s_in,
):
    attn, hb = dk_ref, dq_ref
    c = lax.axis_index("copy")
    d = lax.axis_index("dp")
    f = lax.axis_index("fsdp")
    x, core = d // 2, d % 2
    y, z = f // 8, f % 8
    own = d * 16 + f

    def at_z(step):
        return (c, d, y * 8 + (z + step + 8) % 8)

    def at_x(step):
        return (c, ((x + step + 4) % 4) * 2 + core, f)

    other_y = (c, d, (1 - y) * 8 + z)
    sibling = (c, x * 2 + 1 - core, f)
    partner = (1 - c, d, f)

    def send(src, dst, group, recv, device):
        copy = pltpu.make_async_remote_copy(
            src_ref=src, dst_ref=dst, send_sem=s_send.at[group], recv_sem=recv,
            device_id=device, device_id_type=MESH,
        )
        copy.start()

    def arrived(ref, sem):
        pltpu.make_async_copy(ref, ref, sem).wait()

    loads = [
        pltpu.make_async_copy(src, dst, s_in.at[i])
        for i, (src, dst) in enumerate(
            ((q_hbm, q_ref), (k_hbm, k_ref), (v_hbm, v_ref), (res_hbm, res_ref))
        )
    ]
    for load in loads:
        load.start()

    barrier = pltpu.get_barrier_semaphore()
    greet = (at_z(1), at_z(-1), at_x(1), at_x(-1), at_x(2), other_y, sibling, partner)
    for device in greet:
        pl.semaphore_signal(barrier, inc=1, device_id=device, device_id_type=MESH)
    pl.semaphore_wait(barrier, len(greet))

    STREAMS = ((0, 0, 256), (0, 256, 384), (1, 0, QW), (-1, 0, QW), (2, 0, 384), (2, 384, 256))

    def part_cols(quarter, lo, width):
        return pl.ds(pl.multiple_of(((quarter + 8) % 4) * QW + lo, 128), width)

    def piece(yy, zz, quarter, lo=0, width=QW):
        row = pl.multiple_of((yy * 8 + (zz + 16) % 8) * BLK + core * HALF, 16)
        return wf.at[pl.ds(row, HALF), part_cols(quarter, lo, width)]

    def own_piece(s):
        step, lo, width = STREAMS[s]
        row = pl.ds(pl.multiple_of(core * HALF, 16), HALF)
        return w_ref.at[row, part_cols(x + step, lo, width)]

    def stream_piece(s, yy, zz):
        step, lo, width = STREAMS[s]
        return piece(yy, zz, x + step, lo, width)

    def steps(s, way):
        return 4 if (s + way) % 2 == 0 else 3

    def to_sibling(ref, s):
        send(ref, ref, 0, s_sib.at[s], sibling)

    def z_event(s, k):
        for way, sign in ((0, 1), (1, -1)):
            last = steps(s, way)
            if 0 < k <= last:
                got = stream_piece(s, y, z - sign * k)
                arrived(got, s_zr.at[s, way, k - 1])
                if k < last:
                    send(got, got, 0, s_zr.at[s, way, k], at_z(sign))
                if s < 2:
                    m = NEAR.index(-sign * k) if k < 4 else 7
                    send(got, got, 0, s_yr.at[s, m], other_y)
                to_sibling(got, s)
            elif k == 0:
                dst = stream_piece(s, y, z)
                send(own_piece(s), dst, 0, s_zr.at[s, way, 0], at_z(sign))

    def y_event(s, m):
        got = stream_piece(s, 1 - y, z + NEAR[m])
        arrived(got, s_yr.at[s, m])
        if s == 1:
            both = piece(1 - y, z + NEAR[m], x)
            send(both, both, 0, s_xr.at[0, m], at_x(1))
            send(both, both, 0, s_xr.at[1, m], at_x(-1))
        to_sibling(got, s)

    def x_event(m):
        for way, sign in ((0, 1), (1, -1)):
            got = piece(1 - y, z + NEAR[m], x - sign)
            arrived(got, s_xr.at[way, m])
            if m % 2 == way:
                for i in (0, 1):
                    got_i = piece(1 - y, z + NEAR[m], x - sign, *STREAMS[4 + i][1:])
                    send(got_i, got_i, 0, s_xr.at[way, 8 + 4 * i + m // 2], at_x(sign))
            to_sibling(got, 2 if way == 1 else 3)

    def x_last(n, i):
        for way in (0, 1):
            got = piece(1 - y, z + NEAR[2 * n + way], x + 2, *STREAMS[4 + i][1:])
            arrived(got, s_xr.at[way, 8 + 4 * i + n])
            to_sibling(got, 4 + i)

    for s in (0, 1):
        z_event(s, 0)
        send(own_piece(s), stream_piece(s, y, z), 0, s_yr.at[s, 0], other_y)
    z_event(2, 0)
    send(gain_ref, gp, 1, s_misc.at[0], partner)
    local = pltpu.make_async_copy(
        w_ref, wf.at[pl.ds(pl.multiple_of(f * BLK, 16), BLK), :], s_misc.at[2]
    )
    local.start()

    lane = lax.broadcasted_iota(jnp.int32, (1, 128), 1)
    lens = len_ref[...]
    count = jnp.sum(lens).astype(F32)
    length = jnp.sum(jnp.where(lane == own, lens, 0), axis=-1, keepdims=True)
    r_at = lax.broadcasted_iota(jnp.int32, (L, L), 0)
    c_at = lax.broadcasted_iota(jnp.int32, (L, L), 1)
    bias[...] = jnp.where((c_at <= r_at) & (c_at < length), F32(0.0), F32(-1e30))

    def head(h):
        return pl.ds(pl.multiple_of(h * DH, DH), DH)

    def forward(h, carry):
        cols = head(h)
        s = dot(q_ref[:, cols], k_ref[:, cols], NT) * F32(1.0 / SCALE) + bias[...]
        e = jnp.exp(s - jnp.max(s, axis=-1, keepdims=True))
        p = (e / jnp.sum(e, axis=-1, keepdims=True)).astype(BF16)
        probs[h] = p
        a = dot(p, v_ref[:, cols])
        attn[:, cols] = a.astype(BF16)
        at[cols, 0:L] = a.T.astype(BF16)
        return carry

    def heads(first, n):
        lax.fori_loop(first, first + n, forward, 0)

    for load in loads[:3]:
        load.wait()
    heads(0, 2)
    for k in (1, 2, 3):
        z_event(0, k)
        y_event(0, 2 * k - 2)
        z_event(1, k)
        y_event(1, 2 * k - 2)
        if k == 3:
            z_event(3, 0)
        z_event(2, k)
        heads(6 * k - 4, 3)
        y_event(0, 2 * k - 1)
        y_event(1, 2 * k - 1)
        if k > 1:
            x_event(2 * k - 4)
            x_event(2 * k - 3)
        heads(6 * k - 1, 3)
    z_event(0, 4)
    y_event(0, 6)
    z_event(1, 4)
    y_event(1, 6)
    z_event(3, 1)
    z_event(4, 0)
    z_event(2, 4)
    z_event(5, 0)
    x_event(4)
    y_event(0, 7)
    y_event(1, 7)
    send(at.at[:, 0:L], at.at[:, L : 2 * L], 1, s_misc.at[1], sibling)

    type_at = lax.broadcasted_iota(jnp.int32, (1, 1024), 1).astype(F32)
    ids = jnp.broadcast_to(ids_ref[...].astype(F32), (128, L)).T[:, 0:1]
    looked = jnp.sum(
        jnp.where(ids == type_at, tw_ref[...], F32(0.0)), axis=-1, keepdims=True
    )
    live = lax.broadcasted_iota(jnp.int32, (L, 1), 0) < length
    rows[:, 0:1] = jnp.where(live, looked, F32(0.0))
    rows[:, 1:2] = jnp.zeros((L, 1), F32)
    local.wait()
    loads[3].wait()

    def stream_cols(s):
        step, lo, width = STREAMS[s]
        return part_cols(x + step, lo, width)

    def hidden(s):
        arrived(wf.at[0 : 15 * HALF, 0 : STREAMS[s][2]], s_sib.at[s])
        cols = stream_cols(s)
        hc = res_ref[:, cols].astype(F32) + dot(attn[...], wf[:, cols])
        hid[:, cols] = hc
        hb[:, cols] = hc.astype(BF16)
        rows[:, 1:2] += jnp.sum(hc * hc, axis=-1, keepdims=True)
        if s == 5:
            inv = lax.rsqrt(rows[:, 1:2] * F32(1.0 / D) + F32(1e-06))
            ivs[...] = jnp.broadcast_to(inv, (L, 128)).T[0:8]
            send(ivs, ivr, 1, s_misc.at[4], partner)
        send(hb.at[:, cols], pb.at[:, cols], 2, s_pr.at[s], partner)

    hidden(0)
    z_event(3, 2)
    x_event(5)
    z_event(4, 1)
    z_event(5, 1)
    hidden(1)
    x_event(6)
    z_event(3, 3)
    x_event(7)
    z_event(4, 2)
    z_event(5, 2)
    hidden(2)
    z_event(3, 4)
    z_event(4, 3)
    hidden(3)
    z_event(5, 3)
    for n in range(4):
        x_last(n, 0)
    z_event(4, 4)
    hidden(4)
    for n in range(4):
        x_last(n, 1)
    z_event(5, 4)
    hidden(5)
    arrived(gp, s_misc.at[0])
    arrived(at.at[:, L : 2 * L], s_misc.at[1])
    arrived(ivr, s_misc.at[4])

    tok = rows[:, 0:1]
    inv = lax.rsqrt(rows[:, 1:2] * F32(1.0 / D) + F32(1e-06))
    inv_p = jnp.broadcast_to(ivr[0:1, :], (128, L)).T[:, 0:1]
    coef = 2.0 * tok / (D * count)
    acc[...] = jnp.zeros((2, L, 128), F32)

    for s in range(6):
        arrived(pb.at[:, stream_cols(s)], s_pr.at[s])
        step, lo, width = STREAMS[s]

        def stats(t, carry):
            at_col = ((x + step + 8) % 4) * QW + lo + t * 128
            cols = pl.ds(pl.multiple_of(at_col, 128), 128)
            n = hid[:, cols] * inv
            g = gain_ref[:, cols]
            diff = n * g - pb[:, cols].astype(F32) * inv_p * gp[:, cols]
            acc[0] += diff * diff
            acc[1] += n * (diff * g)
            return carry

        lax.fori_loop(0, width // 128, stats, 0)
    rows[:, 3:4] = jnp.sum(acc[0], axis=-1, keepdims=True)
    rows[:, 4:5] = jnp.sum(acc[1], axis=-1, keepdims=True)
    loss_ref[...] = jnp.sum(tok * rows[:, 3:4], axis=0, keepdims=True) / (D * count)
    mean = rows[:, 4:5] * F32(1.0 / D)

    def grads(t, carry):
        cols = pl.ds(pl.multiple_of(((1 - core) * CW + t * 256) % D, 256), 256)
        n = hid[:, cols] * inv
        g = gain_ref[:, cols]
        diff = n * g - pb[:, cols].astype(F32) * inv_p * gp[:, cols]
        dh[:, cols] = (inv * coef * (diff * g - n * mean)).astype(BF16)
        return carry

    lax.fori_loop(0, 5, grads, 0)
    other_half = pl.ds(pl.multiple_of((1 - core) * CW, 128), CW)
    send(dh.at[:, other_half], dhs, 1, s_misc.at[3], sibling)
    lax.fori_loop(5, 10, grads, 0)
    arrived(dhs, s_misc.at[3])

    def term(row, n_rows, col, width):
        r = pl.ds(pl.multiple_of(row, 16), n_rows)
        mine = dh[:, pl.ds(pl.multiple_of(core * CW + col, 128), width)]
        theirs = dhs[:, pl.ds(pl.multiple_of(col, 128), width)]
        return dot(at[r, 0:L], mine) + dot(at[r, L : 2 * L], theirs)

    def block_row(yy, zz):
        return (yy * 8 + (zz + 16) % 8) * BLK

    WAYS = ((0, 1), (1, -1))

    def b_first(t):
        for way, sign in WAYS:
            for yy in (0, 1):
                val = term(block_row(yy, z - sign * (1 + t)), BLK, 2 * AW + way * BW, BW)
                pbuf[way, t, :, yy] = val.reshape(4, 40, BW).astype(BF16)
            send(
                pbuf.at[way, t, (x - sign + 4) % 4], xb.at[way, 0, t], 4,
                s_xb.at[way, 0, t], at_x(sign),
            )

    def b_next(t, k):
        for way, sign in WAYS:
            slot = xb.at[way, k - 1, t]
            arrived(slot, s_xb.at[way, k - 1, t])
            mine = pbuf[way, t, (x - sign * (1 + k) + 8) % 4]
            slot[...] = (slot[...].astype(F32) + mine.astype(F32)).astype(BF16)
            send(slot, xb.at[way, k, t], 4, s_xb.at[way, k, t], at_x(sign))

    def b_sum(way, t):
        slot = xb.at[way, 2, t]
        arrived(slot, s_xb.at[way, 2, t])
        return slot[...].astype(F32) + pbuf[way, t, x].astype(F32)

    def b_z(t):
        for way, sign in WAYS:
            val = b_sum(way, t)
            slot = zb.at[way, t]

            @pl.when(t == 0)
            def _():
                slot[...] = val.astype(BF16)

            @pl.when(t > 0)
            def _():
                arrived(slot, s_zb.at[way, t])
                slot[...] = (slot[...].astype(F32) + val).astype(BF16)

            send(slot, zb.at[way, t + 1], 5, s_zb.at[way, t + 1], at_z(sign))

    def a_step(t, yy):
        hop, part = t // 2, t % 2
        for way, sign in WAYS:
            n = steps(yy, way)

            @pl.when(t < 2 * n)
            def _():
                val = term(block_row(yy, z + sign * (n - hop)), BLK, part * AW, AW)
                slot = za.at[way, yy, part, hop]

                @pl.when(hop == 0)
                def _():
                    slot[...] = val.astype(BF16)

                @pl.when(hop > 0)
                def _():
                    arrived(slot, s_za.at[way, yy, part, hop])
                    slot[...] = (slot[...].astype(F32) + val).astype(BF16)

                send(
                    slot, za.at[way, yy, part, hop + 1], 3,
                    s_za.at[way, yy, part, hop + 1], at_z(sign),
                )

    def a_last(part):
        for yy in (0, 1):
            val = term(block_row(yy, z), BLK, part * AW, AW)
            for way in (0, 1):
                n = steps(yy, way)
                slot = za.at[way, yy, part, n]
                arrived(slot, s_za.at[way, yy, part, n])
                val = val + slot[...].astype(F32)
            zaf[part, :, yy] = val.reshape(4, 40, AW).astype(BF16)
        sign = 1 - 2 * part
        send(zaf.at[part, (x - sign + 4) % 4], xa.at[part, 0], 6, s_xa.at[part, 0], at_x(sign))

    def a_next(way, k):
        sign = 1 - 2 * way
        slot = xa.at[way, k - 1]
        arrived(slot, s_xa.at[way, k - 1])
        mine = zaf[way, (x - sign * (1 + k) + 8) % 4]
        slot[...] = (slot[...].astype(F32) + mine.astype(F32)).astype(BF16)
        send(slot, xa.at[way, k], 6, s_xa.at[way, k], at_x(sign))

    def pair_in(t):
        cols2 = pl.ds(pl.multiple_of(t * 256, 256), 256)
        dab[...] = dot(dh[...], wf[cols2, :], NT).astype(BF16)

    def pair(t, j):
        if True:
            cols = pl.ds(pl.multiple_of(t * 256 + j * DH, DH), DH)
            da = dab[:, j * DH : (j + 1) * DH]
            p = probs[2 * t + j]
            dv_ref[:, cols] = dot(p, da, TN).astype(BF16)
            dprob = dot(da, v_ref[:, cols], NT)
            pf = p.astype(F32)
            delta = jnp.sum(dprob * pf, axis=-1, keepdims=True)
            ds = (pf * (dprob - delta) * F32(1.0 / SCALE)).astype(BF16)
            dq_ref[:, cols] = dot(ds, k_ref[:, cols]).astype(BF16)
            dk_ref[:, cols] = dot(ds, q_ref[:, cols], TN).astype(BF16)

    arrived(pb, s_send.at[2])

    def tick(t, carry):
        @pl.when(t < 8)
        def _():
            a_step(t, 0)
            b_first(t)

        @pl.when(t == 8)
        def _():
            a_last(1)
            a_next(0, 1)

        @pl.when(t == 9)
        def _():
            a_next(0, 2)
            a_next(1, 1)

        pair_in(t)

        @pl.when(t < 8)
        def _():
            a_step(t, 1)

        @pl.when(t == 7)
        def _():
            a_last(0)

        @pl.when((t >= 1) & (t < 9))
        def _():
            b_next(t - 1, 1)

        pair(t, 0)

        @pl.when((t >= 2) & (t < 10))
        def _():
            b_next(t - 2, 2)

        @pl.when((t >= 3) & (t < 10))
        def _():
            b_z(t - 3)

        pair(t, 1)
        return carry

    lax.fori_loop(0, 10, tick, 0)
    a_next(1, 2)

    PARTS = ((0, 2 * AW), (2 * AW, 2 * BW))

    def to_y(part):
        lo, width = PARTS[part]
        send(
            fsum.at[1 - y, :, lo : lo + width], yrx.at[:, lo : lo + width], 7,
            s_fin.at[part, 0], other_y,
        )

    def place(part, quarter, of_core):
        lo, width = PARTS[part]
        cols = pl.ds(pl.multiple_of(of_core * CW + lo, 128), width)
        return dwo_ref.at[(quarter + 4) % 4, :, cols]

    def from_y(part):
        lo, width = PARTS[part]
        got = yrx.at[:, lo : lo + width]
        arrived(got, s_fin.at[part, 0])
        mine = place(part, x, core)
        mine[...] = (got[...].astype(F32) + fsum[y, :, lo : lo + width].astype(F32)).astype(BF16)
        for i, step in enumerate((1, -1, 2)):
            send(mine, mine, 7, s_fin.at[part, 1 + i], at_x(step))
        send(mine, mine, 7, s_fin.at[part, 4], sibling)

    def from_x(part):
        for i, step in enumerate((1, -1, 2)):
            got = place(part, x - step, core)
            arrived(got, s_fin.at[part, 1 + i])
            send(got, got, 7, s_fin.at[part, 5 + i], sibling)

    def from_sibling(part):
        for i, step in enumerate((0, 1, -1, 2)):
            arrived(place(part, x - step, 1 - core), s_fin.at[part, 4 + i])

    for way, sign in WAYS:
        slot = xa.at[way, 2]
        arrived(slot, s_xa.at[way, 2])
        val = slot[...].astype(F32) + zaf[way, x].astype(F32)
        fsum[:, :, way * AW : (way + 1) * AW] = val.astype(BF16)
    to_y(0)
    for way, sign in WAYS:
        val = b_sum(way, 7)
        slot = zb.at[way, 7]
        arrived(slot, s_zb.at[way, 7])
        lo = 2 * AW + way * BW
        fsum[:, :, lo : lo + BW] = (slot[...].astype(F32) + val).astype(BF16)
    to_y(1)
    from_y(0)
    from_y(1)
    from_x(0)
    from_x(1)
    from_sibling(0)
    from_sibling(1)

    arrived(wf.at[0 : 32 * HALF, 0:QW], s_send.at[0])
    arrived(wf.at[0 : 32 * HALF, 0:QW], s_send.at[0])
    arrived(wf.at[0 : 32 * HALF, 0:QW], s_send.at[0])
    arrived(wf.at[0 : 24 * HALF, 0:QW], s_send.at[0])
    arrived(gp, s_send.at[1])
    arrived(ivr, s_send.at[1])
    arrived(at.at[:, 0:L], s_send.at[1])
    arrived(dhs, s_send.at[1])
    for way in (0, 1):
        for yy in (0, 1):
            arrived(za.at[way, yy, :, 1 : steps(yy, way) + 1], s_send.at[3])
        arrived(xb.at[way], s_send.at[4])
        arrived(zb.at[way, 1:8], s_send.at[5])
        arrived(xa.at[way], s_send.at[6])
    for _ in range(8):
        arrived(yrx, s_send.at[7])


def finish(
    loss_in, dq, dk, dv, dwo, loss_out, dq_out, dk_out, dv_out, dwo_out, dwo_f, s_out
):
    given = []
    for i, (src, dst) in enumerate(((dq, dq_out), (dk, dk_out), (dv, dv_out), (dwo_f, dwo_out))):
        if i == 3:
            dwo_f[...] = dwo[...].astype(F32).reshape(BLK, D)
        given.append(pltpu.make_async_copy(src, dst, s_out.at[i]))
        given[-1].start()
    loss_out[...] = loss_in[...]
    for copy in given:
        copy.wait()


def body(queries, keys, values, residual, event_ids, lengths, type_weight, w_out, gain):
    vmem = pl.BlockSpec(memory_space=pltpu.VMEM)
    hbm = pl.BlockSpec(memory_space=pl.ANY)
    dma = pltpu.SemaphoreType.DMA
    big = jax.ShapeDtypeStruct((L, D), BF16)
    near = pltpu.VMEM((L, D), BF16)
    loss, dq, dk, dv, dwo = pl.pallas_call(
        kernel,
        out_shape=(
            jax.ShapeDtypeStruct((1, 1), F32), near, near, near,
            pltpu.VMEM((4, 40, D), BF16),
        ),
        in_specs=[hbm] * 5 + [vmem] * 4,
        out_specs=(vmem,) * 5,
        scratch_shapes=[pltpu.VMEM((L, D), BF16)] * 4
        + [
            pltpu.VMEM((D, D), BF16),
            pltpu.VMEM((D, 2 * L), BF16),
            pltpu.VMEM((L, D), F32),
            pltpu.VMEM((L, D), BF16),
            pltpu.VMEM((1, D), F32),
            pltpu.VMEM((L, D), BF16),
            pltpu.VMEM((L, CW), BF16),
            pltpu.VMEM((H, L, L), BF16),
            pltpu.VMEM((L, L), F32),
            pltpu.VMEM((2, 8, 4, 2, 40, BW), BF16),
            pltpu.VMEM((2, 2, 2, 5, BLK, AW), BF16),
            pltpu.VMEM((2, 4, 2, 40, AW), BF16),
            pltpu.VMEM((2, 3, 2, 40, AW), BF16),
            pltpu.VMEM((2, 3, 8, 2, 40, BW), BF16),
            pltpu.VMEM((2, 8, 2, 40, BW), BF16),
            pltpu.VMEM((2, 40, CW), BF16),
            pltpu.VMEM((40, CW), BF16),
            pltpu.VMEM((L, 128), F32),
            pltpu.VMEM((L, 256), BF16),
            pltpu.VMEM((8, L), F32),
            pltpu.VMEM((8, L), F32),
            pltpu.VMEM((2, L, 128), F32),
            dma((8,)),
            dma((6, 2, 4)),
            dma((2, 16)),
            dma((2, 8)),
            dma((6,)),
            dma((6,)),
            dma((5,)),
            dma((2, 2, 2, 5)),
            dma((2, 3)),
            dma((2, 3, 8)),
            dma((2, 8)),
            dma((2, 8)),
            dma((4,)),
        ],
        compiler_params=pltpu.CompilerParams(
            collective_id=0, has_side_effects=True, vmem_limit_bytes=58 * 1024 * 1024
        ),
        name="step",
    )(
        queries[0, 0], keys[0, 0], values[0, 0], residual[0, 0], w_out[0],
        event_ids, lengths.reshape(1, 128), type_weight.reshape(1, 1024), gain,
    )
    loss, dq, dk, dv, dwo = pl.pallas_call(
        finish,
        out_shape=(
            jax.ShapeDtypeStruct((1, 1), F32), big, big, big, jax.ShapeDtypeStruct((BLK, D), F32)
        ),
        in_specs=[vmem] * 5,
        out_specs=(vmem, hbm, hbm, hbm, hbm),
        scratch_shapes=[pltpu.VMEM((BLK, D), F32), dma((4,))],
        compiler_params=pltpu.CompilerParams(vmem_limit_bytes=4 * 1024 * 1024),
        name="finish",
    )(loss, dq, dk, dv, dwo)
    return loss, dq[None, None], dk[None, None], dv[None, None], dwo[None]


def solution(mesh):
    hist = P("copy", ("dp", "fsdp"), None, None)
    return jax.shard_map(
        body,
        mesh=mesh,
        in_specs=(
            hist, hist, hist, hist, P(("dp", "fsdp"), None), P(), P(),
            P("copy", "fsdp", None), P("copy", None),
        ),
        out_specs=(
            P("copy", ("dp", "fsdp")), hist, hist, hist, P("copy", "fsdp", None),
        ),
        check_vma=False,
    )
```

```python
import jax
import jax.numpy as jnp
from jax import lax
from jax.experimental import pallas as pl
from jax.experimental.pallas import tpu as pltpu
from jax.sharding import PartitionSpec as P

MESH = pl.DeviceIdType.MESH
F32 = jnp.float32
BF16 = jnp.bfloat16
L, D, H, DH = 256, 2560, 20, 128
BLK = 160
HALF = 80
QW = 640
CW = 1280
AW, BW = 256, 384
SCALE = 128.0**0.5
NT = (((1,), (1,)), ((), ()))
TN = (((0,), (0,)), ((), ()))
NEAR = (0, -1, 1, -2, 2, -3, 3, -4)


def dot(a, b, dims=(((1,), (0,)), ((), ()))):
    return lax.dot_general(a, b, dims, preferred_element_type=F32)


def kernel(
    q_hbm, k_hbm, v_hbm, res_hbm, w_ref, ids_ref, len_ref, tw_ref, gain_ref,
    loss_ref, dq_ref, dk_ref, dv_ref, dwo_ref,
    q_ref, k_ref, v_ref, res_ref, wf, at, hid, pb, gp, dh, dhs, probs, bias, pbuf, za, zaf, xa, xb, zb, fsum, yrx, rows, dab, ivs, ivr, acc,
    s_send, s_zr, s_xr, s_yr, s_sib, s_pr, s_misc, s_za, s_xa, s_xb, s_zb, s_fin, s_in,
):
    attn, hb = dk_ref, dq_ref
    c = lax.axis_index("copy")
    d = lax.axis_index("dp")
    f = lax.axis_index("fsdp")
    x, core = d // 2, d % 2
    y, z = f // 8, f % 8
    own = d * 16 + f

    def at_z(step):
        return (c, d, y * 8 + (z + step + 8) % 8)

    def at_x(step):
        return (c, ((x + step + 4) % 4) * 2 + core, f)

    other_y = (c, d, (1 - y) * 8 + z)
    sibling = (c, x * 2 + 1 - core, f)
    partner = (1 - c, d, f)

    def send(src, dst, group, recv, device):
        copy = pltpu.make_async_remote_copy(
            src_ref=src, dst_ref=dst, send_sem=s_send.at[group], recv_sem=recv,
            device_id=device, device_id_type=MESH,
        )
        copy.start()

    def arrived(ref, sem):
        pltpu.make_async_copy(ref, ref, sem).wait()

    loads = [
        pltpu.make_async_copy(src, dst, s_in.at[i])
        for i, (src, dst) in enumerate(
            ((q_hbm, q_ref), (k_hbm, k_ref), (v_hbm, v_ref), (res_hbm, res_ref))
        )
    ]
    for load in loads:
        load.start()

    barrier = pltpu.get_barrier_semaphore()
    greet = (at_z(1), at_z(-1), at_x(1), at_x(-1), at_x(2), other_y, sibling, partner)
    for device in greet:
        pl.semaphore_signal(barrier, inc=1, device_id=device, device_id_type=MESH)
    pl.semaphore_wait(barrier, len(greet))

    STREAMS = ((0, 0, 256), (0, 256, 384), (1, 0, QW), (-1, 0, QW), (2, 0, 384), (2, 384, 256))

    def part_cols(quarter, lo, width):
        return pl.ds(pl.multiple_of(((quarter + 8) % 4) * QW + lo, 128), width)

    def piece(yy, zz, quarter, lo=0, width=QW):
        row = pl.multiple_of((yy * 8 + (zz + 16) % 8) * BLK + core * HALF, 16)
        return wf.at[pl.ds(row, HALF), part_cols(quarter, lo, width)]

    def own_piece(s):
        step, lo, width = STREAMS[s]
        row = pl.ds(pl.multiple_of(core * HALF, 16), HALF)
        return w_ref.at[row, part_cols(x + step, lo, width)]

    def stream_piece(s, yy, zz):
        step, lo, width = STREAMS[s]
        return piece(yy, zz, x + step, lo, width)

    def steps(s, way):
        return 4 if (s + way) % 2 == 0 else 3

    def to_sibling(ref, s):
        send(ref, ref, 0, s_sib.at[s], sibling)

    def z_event(s, k):
        for way, sign in ((0, 1), (1, -1)):
            last = steps(s, way)
            if 0 < k <= last:
                got = stream_piece(s, y, z - sign * k)
                arrived(got, s_zr.at[s, way, k - 1])
                if k < last:
                    send(got, got, 0, s_zr.at[s, way, k], at_z(sign))
                if s < 2:
                    m = NEAR.index(-sign * k) if k < 4 else 7
                    send(got, got, 0, s_yr.at[s, m], other_y)
                to_sibling(got, s)
            elif k == 0:
                dst = stream_piece(s, y, z)
                send(own_piece(s), dst, 0, s_zr.at[s, way, 0], at_z(sign))

    def y_event(s, m):
        got = stream_piece(s, 1 - y, z + NEAR[m])
        arrived(got, s_yr.at[s, m])
        if s == 1:
            both = piece(1 - y, z + NEAR[m], x)
            send(both, both, 0, s_xr.at[0, m], at_x(1))
            send(both, both, 0, s_xr.at[1, m], at_x(-1))
        to_sibling(got, s)

    def x_event(m):
        for way, sign in ((0, 1), (1, -1)):
            got = piece(1 - y, z + NEAR[m], x - sign)
            arrived(got, s_xr.at[way, m])
            if m % 2 == way:
                for i in (0, 1):
                    got_i = piece(1 - y, z + NEAR[m], x - sign, *STREAMS[4 + i][1:])
                    send(got_i, got_i, 0, s_xr.at[way, 8 + 4 * i + m // 2], at_x(sign))
            to_sibling(got, 2 if way == 1 else 3)

    def x_last(n, i):
        for way in (0, 1):
            got = piece(1 - y, z + NEAR[2 * n + way], x + 2, *STREAMS[4 + i][1:])
            arrived(got, s_xr.at[way, 8 + 4 * i + n])
            to_sibling(got, 4 + i)

    for s in (0, 1):
        z_event(s, 0)
        send(own_piece(s), stream_piece(s, y, z), 0, s_yr.at[s, 0], other_y)
    z_event(2, 0)
    send(gain_ref, gp, 1, s_misc.at[0], partner)
    local = pltpu.make_async_copy(
        w_ref, wf.at[pl.ds(pl.multiple_of(f * BLK, 16), BLK), :], s_misc.at[2]
    )
    local.start()

    lane = lax.broadcasted_iota(jnp.int32, (1, 128), 1)
    lens = len_ref[...]
    count = jnp.sum(lens).astype(F32)
    length = jnp.sum(jnp.where(lane == own, lens, 0), axis=-1, keepdims=True)
    r_at = lax.broadcasted_iota(jnp.int32, (L, L), 0)
    c_at = lax.broadcasted_iota(jnp.int32, (L, L), 1)
    bias[...] = jnp.where((c_at <= r_at) & (c_at < length), F32(0.0), F32(-1e30))

    def head(h):
        return pl.ds(pl.multiple_of(h * DH, DH), DH)

    def forward(h, carry):
        cols = head(h)
        s = dot(q_ref[:, cols], k_ref[:, cols], NT) * F32(1.0 / SCALE) + bias[...]
        e = jnp.exp(s - jnp.max(s, axis=-1, keepdims=True))
        p = (e / jnp.sum(e, axis=-1, keepdims=True)).astype(BF16)
        probs[h] = p
        a = dot(p, v_ref[:, cols])
        attn[:, cols] = a.astype(BF16)
        at[cols, 0:L] = a.T.astype(BF16)
        return carry

    def heads(first, n):
        lax.fori_loop(first, first + n, forward, 0)

    for load in loads[:3]:
        load.wait()
    heads(0, 2)
    for k in (1, 2, 3):
        z_event(0, k)
        y_event(0, 2 * k - 2)
        z_event(1, k)
        y_event(1, 2 * k - 2)
        if k == 3:
            z_event(3, 0)
        z_event(2, k)
        heads(6 * k - 4, 3)
        y_event(0, 2 * k - 1)
        y_event(1, 2 * k - 1)
        if k > 1:
            x_event(2 * k - 4)
            x_event(2 * k - 3)
        heads(6 * k - 1, 3)
    z_event(0, 4)
    y_event(0, 6)
    z_event(1, 4)
    y_event(1, 6)
    z_event(3, 1)
    z_event(4, 0)
    z_event(2, 4)
    z_event(5, 0)
    x_event(4)
    y_event(0, 7)
    y_event(1, 7)
    send(at.at[:, 0:L], at.at[:, L : 2 * L], 1, s_misc.at[1], sibling)

    type_at = lax.broadcasted_iota(jnp.int32, (1, 1024), 1).astype(F32)
    ids = jnp.broadcast_to(ids_ref[...].astype(F32), (128, L)).T[:, 0:1]
    looked = jnp.sum(
        jnp.where(ids == type_at, tw_ref[...], F32(0.0)), axis=-1, keepdims=True
    )
    live = lax.broadcasted_iota(jnp.int32, (L, 1), 0) < length
    rows[:, 0:1] = jnp.where(live, looked, F32(0.0))
    rows[:, 1:2] = jnp.zeros((L, 1), F32)
    local.wait()
    loads[3].wait()

    def stream_cols(s):
        step, lo, width = STREAMS[s]
        return part_cols(x + step, lo, width)

    def hidden(s):
        arrived(wf.at[0 : 15 * HALF, 0 : STREAMS[s][2]], s_sib.at[s])
        cols = stream_cols(s)
        hc = res_ref[:, cols].astype(F32) + dot(attn[...], wf[:, cols])
        hid[:, cols] = hc
        hb[:, cols] = hc.astype(BF16)
        rows[:, 1:2] += jnp.sum(hc * hc, axis=-1, keepdims=True)
        if s == 5:
            inv = lax.rsqrt(rows[:, 1:2] * F32(1.0 / D) + F32(1e-06))
            ivs[...] = jnp.broadcast_to(inv, (L, 128)).T[0:8]
            send(ivs, ivr, 1, s_misc.at[4], partner)
        send(hb.at[:, cols], pb.at[:, cols], 2, s_pr.at[s], partner)

    hidden(0)
    z_event(3, 2)
    x_event(5)
    z_event(4, 1)
    z_event(5, 1)
    hidden(1)
    x_event(6)
    z_event(3, 3)
    x_event(7)
    z_event(4, 2)
    z_event(5, 2)
    hidden(2)
    z_event(3, 4)
    z_event(4, 3)
    hidden(3)
    z_event(5, 3)
    for n in range(4):
        x_last(n, 0)
    z_event(4, 4)
    hidden(4)
    for n in range(4):
        x_last(n, 1)
    z_event(5, 4)
    hidden(5)
    arrived(gp, s_misc.at[0])
    arrived(at.at[:, L : 2 * L], s_misc.at[1])
    arrived(ivr, s_misc.at[4])

    tok = rows[:, 0:1]
    inv = lax.rsqrt(rows[:, 1:2] * F32(1.0 / D) + F32(1e-06))
    inv_p = jnp.broadcast_to(ivr[0:1, :], (128, L)).T[:, 0:1]
    coef = 2.0 * tok / (D * count)
    acc[...] = jnp.zeros((2, L, 128), F32)

    for s in range(6):
        arrived(pb.at[:, stream_cols(s)], s_pr.at[s])
        step, lo, width = STREAMS[s]

        def stats(t, carry):
            at_col = ((x + step + 8) % 4) * QW + lo + t * 128
            cols = pl.ds(pl.multiple_of(at_col, 128), 128)
            n = hid[:, cols] * inv
            g = gain_ref[:, cols]
            diff = n * g - pb[:, cols].astype(F32) * inv_p * gp[:, cols]
            acc[0] += diff * diff
            acc[1] += n * (diff * g)
            return carry

        lax.fori_loop(0, width // 128, stats, 0)
    rows[:, 3:4] = jnp.sum(acc[0], axis=-1, keepdims=True)
    rows[:, 4:5] = jnp.sum(acc[1], axis=-1, keepdims=True)
    loss_ref[...] = jnp.sum(tok * rows[:, 3:4], axis=0, keepdims=True) / (D * count)
    mean = rows[:, 4:5] * F32(1.0 / D)

    def grads(t, carry):
        cols = pl.ds(pl.multiple_of(((1 - core) * CW + t * 256) % D, 256), 256)
        n = hid[:, cols] * inv
        g = gain_ref[:, cols]
        diff = n * g - pb[:, cols].astype(F32) * inv_p * gp[:, cols]
        dh[:, cols] = (inv * coef * (diff * g - n * mean)).astype(BF16)
        return carry

    lax.fori_loop(0, 5, grads, 0)
    other_half = pl.ds(pl.multiple_of((1 - core) * CW, 128), CW)
    send(dh.at[:, other_half], dhs, 1, s_misc.at[3], sibling)
    lax.fori_loop(5, 10, grads, 0)
    arrived(dhs, s_misc.at[3])

    def term(row, n_rows, col, width):
        r = pl.ds(pl.multiple_of(row, 16), n_rows)
        mine = dh[:, pl.ds(pl.multiple_of(core * CW + col, 128), width)]
        theirs = dhs[:, pl.ds(pl.multiple_of(col, 128), width)]
        return dot(at[r, 0:L], mine) + dot(at[r, L : 2 * L], theirs)

    def block_row(yy, zz):
        return (yy * 8 + (zz + 16) % 8) * BLK

    WAYS = ((0, 1), (1, -1))

    def b_first(t):
        for way, sign in WAYS:
            for yy in (0, 1):
                val = term(block_row(yy, z - sign * (1 + t)), BLK, 2 * AW + way * BW, BW)
                pbuf[way, t, :, yy] = val.reshape(4, 40, BW).astype(BF16)
            send(
                pbuf.at[way, t, (x - sign + 4) % 4], xb.at[way, 0, t], 4,
                s_xb.at[way, 0, t], at_x(sign),
            )

    def b_next(t, k):
        for way, sign in WAYS:
            slot = xb.at[way, k - 1, t]
            arrived(slot, s_xb.at[way, k - 1, t])
            mine = pbuf[way, t, (x - sign * (1 + k) + 8) % 4]
            slot[...] = (slot[...].astype(F32) + mine.astype(F32)).astype(BF16)
            send(slot, xb.at[way, k, t], 4, s_xb.at[way, k, t], at_x(sign))

    def b_sum(way, t):
        slot = xb.at[way, 2, t]
        arrived(slot, s_xb.at[way, 2, t])
        return slot[...].astype(F32) + pbuf[way, t, x].astype(F32)

    def b_z(t):
        for way, sign in WAYS:
            val = b_sum(way, t)
            slot = zb.at[way, t]

            @pl.when(t == 0)
            def _():
                slot[...] = val.astype(BF16)

            @pl.when(t > 0)
            def _():
                arrived(slot, s_zb.at[way, t])
                slot[...] = (slot[...].astype(F32) + val).astype(BF16)

            send(slot, zb.at[way, t + 1], 5, s_zb.at[way, t + 1], at_z(sign))

    def a_step(t, yy):
        hop, part = t // 2, t % 2
        for way, sign in WAYS:
            n = steps(yy, way)

            @pl.when(t < 2 * n)
            def _():
                val = term(block_row(yy, z + sign * (n - hop)), BLK, part * AW, AW)
                slot = za.at[way, yy, part, hop]

                @pl.when(hop == 0)
                def _():
                    slot[...] = val.astype(BF16)

                @pl.when(hop > 0)
                def _():
                    arrived(slot, s_za.at[way, yy, part, hop])
                    slot[...] = (slot[...].astype(F32) + val).astype(BF16)

                send(
                    slot, za.at[way, yy, part, hop + 1], 3,
                    s_za.at[way, yy, part, hop + 1], at_z(sign),
                )

    def a_last(part):
        for yy in (0, 1):
            val = term(block_row(yy, z), BLK, part * AW, AW)
            for way in (0, 1):
                n = steps(yy, way)
                slot = za.at[way, yy, part, n]
                arrived(slot, s_za.at[way, yy, part, n])
                val = val + slot[...].astype(F32)
            zaf[part, :, yy] = val.reshape(4, 40, AW).astype(BF16)
        sign = 1 - 2 * part
        send(zaf.at[part, (x - sign + 4) % 4], xa.at[part, 0], 6, s_xa.at[part, 0], at_x(sign))

    def a_next(way, k):
        sign = 1 - 2 * way
        slot = xa.at[way, k - 1]
        arrived(slot, s_xa.at[way, k - 1])
        mine = zaf[way, (x - sign * (1 + k) + 8) % 4]
        slot[...] = (slot[...].astype(F32) + mine.astype(F32)).astype(BF16)
        send(slot, xa.at[way, k], 6, s_xa.at[way, k], at_x(sign))

    def pair_in(t):
        cols2 = pl.ds(pl.multiple_of(t * 256, 256), 256)
        dab[...] = dot(dh[...], wf[cols2, :], NT).astype(BF16)

    def pair(t, j):
        if True:
            cols = pl.ds(pl.multiple_of(t * 256 + j * DH, DH), DH)
            da = dab[:, j * DH : (j + 1) * DH]
            p = probs[2 * t + j]
            dv_ref[:, cols] = dot(p, da, TN).astype(BF16)
            dprob = dot(da, v_ref[:, cols], NT)
            pf = p.astype(F32)
            delta = jnp.sum(dprob * pf, axis=-1, keepdims=True)
            ds = (pf * (dprob - delta) * F32(1.0 / SCALE)).astype(BF16)
            dq_ref[:, cols] = dot(ds, k_ref[:, cols]).astype(BF16)
            dk_ref[:, cols] = dot(ds, q_ref[:, cols], TN).astype(BF16)

    arrived(pb, s_send.at[2])

    def tick(t, carry):
        @pl.when(t < 8)
        def _():
            a_step(t, 0)
            b_first(t)

        @pl.when(t == 8)
        def _():
            a_last(1)
            a_next(0, 1)

        @pl.when(t == 9)
        def _():
            a_next(0, 2)
            a_next(1, 1)

        @pl.when(t < 8)
        def _():
            pair_in(t)

        @pl.when(t < 8)
        def _():
            a_step(t, 1)

        @pl.when(t == 7)
        def _():
            a_last(0)

        @pl.when(t < 8)
        def _():
            pair(t, 0)

        @pl.when((t >= 1) & (t < 9))
        def _():
            b_next(t - 1, 1)

        @pl.when(t < 8)
        def _():
            pair(t, 1)

        @pl.when((t >= 2) & (t < 10))
        def _():
            b_next(t - 2, 2)

        @pl.when((t >= 3) & (t < 10))
        def _():
            b_z(t - 3)

        return carry

    lax.fori_loop(0, 10, tick, 0)
    a_next(1, 2)

    PARTS = ((0, 2 * AW), (2 * AW, 2 * BW))

    def to_y(part):
        lo, width = PARTS[part]
        send(
            fsum.at[1 - y, :, lo : lo + width], yrx.at[:, lo : lo + width], 7,
            s_fin.at[part, 0], other_y,
        )

    def place(part, quarter, of_core):
        lo, width = PARTS[part]
        cols = pl.ds(pl.multiple_of(of_core * CW + lo, 128), width)
        return dwo_ref.at[(quarter + 4) % 4, :, cols]

    def from_y(part):
        lo, width = PARTS[part]
        got = yrx.at[:, lo : lo + width]
        arrived(got, s_fin.at[part, 0])
        mine = place(part, x, core)
        mine[...] = (got[...].astype(F32) + fsum[y, :, lo : lo + width].astype(F32)).astype(BF16)
        for i, step in enumerate((1, -1, 2)):
            send(mine, mine, 7, s_fin.at[part, 1 + i], at_x(step))
        send(mine, mine, 7, s_fin.at[part, 4], sibling)

    def from_x(part):
        for i, step in enumerate((1, -1, 2)):
            got = place(part, x - step, core)
            arrived(got, s_fin.at[part, 1 + i])
            send(got, got, 7, s_fin.at[part, 5 + i], sibling)

    def from_sibling(part):
        for i, step in enumerate((0, 1, -1, 2)):
            arrived(place(part, x - step, 1 - core), s_fin.at[part, 4 + i])

    for way, sign in WAYS:
        slot = xa.at[way, 2]
        arrived(slot, s_xa.at[way, 2])
        val = slot[...].astype(F32) + zaf[way, x].astype(F32)
        fsum[:, :, way * AW : (way + 1) * AW] = val.astype(BF16)
    to_y(0)
    for way, sign in WAYS:
        val = b_sum(way, 7)
        slot = zb.at[way, 7]
        arrived(slot, s_zb.at[way, 7])
        lo = 2 * AW + way * BW
        fsum[:, :, lo : lo + BW] = (slot[...].astype(F32) + val).astype(BF16)
    to_y(1)
    pair_in(8)
    pair(8, 0)
    from_y(0)
    pair(8, 1)
    from_y(1)
    pair_in(9)
    pair(9, 0)
    pair(9, 1)
    from_x(0)
    from_x(1)
    from_sibling(0)
    from_sibling(1)

    arrived(wf.at[0 : 32 * HALF, 0:QW], s_send.at[0])
    arrived(wf.at[0 : 32 * HALF, 0:QW], s_send.at[0])
    arrived(wf.at[0 : 32 * HALF, 0:QW], s_send.at[0])
    arrived(wf.at[0 : 24 * HALF, 0:QW], s_send.at[0])
    arrived(gp, s_send.at[1])
    arrived(ivr, s_send.at[1])
    arrived(at.at[:, 0:L], s_send.at[1])
    arrived(dhs, s_send.at[1])
    for way in (0, 1):
        for yy in (0, 1):
            arrived(za.at[way, yy, :, 1 : steps(yy, way) + 1], s_send.at[3])
        arrived(xb.at[way], s_send.at[4])
        arrived(zb.at[way, 1:8], s_send.at[5])
        arrived(xa.at[way], s_send.at[6])
    for _ in range(8):
        arrived(yrx, s_send.at[7])


def finish(
    loss_in, dq, dk, dv, dwo, loss_out, dq_out, dk_out, dv_out, dwo_out, dwo_f, s_out
):
    given = []
    for i, (src, dst) in enumerate(((dq, dq_out), (dk, dk_out), (dv, dv_out), (dwo_f, dwo_out))):
        if i == 3:
            dwo_f[...] = dwo[...].astype(F32).reshape(BLK, D)
        given.append(pltpu.make_async_copy(src, dst, s_out.at[i]))
        given[-1].start()
    loss_out[...] = loss_in[...]
    for copy in given:
        copy.wait()


def body(queries, keys, values, residual, event_ids, lengths, type_weight, w_out, gain):
    vmem = pl.BlockSpec(memory_space=pltpu.VMEM)
    hbm = pl.BlockSpec(memory_space=pl.ANY)
    dma = pltpu.SemaphoreType.DMA
    big = jax.ShapeDtypeStruct((L, D), BF16)
    near = pltpu.VMEM((L, D), BF16)
    loss, dq, dk, dv, dwo = pl.pallas_call(
        kernel,
        out_shape=(
            jax.ShapeDtypeStruct((1, 1), F32), near, near, near,
            pltpu.VMEM((4, 40, D), BF16),
        ),
        in_specs=[hbm] * 5 + [vmem] * 4,
        out_specs=(vmem,) * 5,
        scratch_shapes=[pltpu.VMEM((L, D), BF16)] * 4
        + [
            pltpu.VMEM((D, D), BF16),
            pltpu.VMEM((D, 2 * L), BF16),
            pltpu.VMEM((L, D), F32),
            pltpu.VMEM((L, D), BF16),
            pltpu.VMEM((1, D), F32),
            pltpu.VMEM((L, D), BF16),
            pltpu.VMEM((L, CW), BF16),
            pltpu.VMEM((H, L, L), BF16),
            pltpu.VMEM((L, L), F32),
            pltpu.VMEM((2, 8, 4, 2, 40, BW), BF16),
            pltpu.VMEM((2, 2, 2, 5, BLK, AW), BF16),
            pltpu.VMEM((2, 4, 2, 40, AW), BF16),
            pltpu.VMEM((2, 3, 2, 40, AW), BF16),
            pltpu.VMEM((2, 3, 8, 2, 40, BW), BF16),
            pltpu.VMEM((2, 8, 2, 40, BW), BF16),
            pltpu.VMEM((2, 40, CW), BF16),
            pltpu.VMEM((40, CW), BF16),
            pltpu.VMEM((L, 128), F32),
            pltpu.VMEM((L, 256), BF16),
            pltpu.VMEM((8, L), F32),
            pltpu.VMEM((8, L), F32),
            pltpu.VMEM((2, L, 128), F32),
            dma((8,)),
            dma((6, 2, 4)),
            dma((2, 16)),
            dma((2, 8)),
            dma((6,)),
            dma((6,)),
            dma((5,)),
            dma((2, 2, 2, 5)),
            dma((2, 3)),
            dma((2, 3, 8)),
            dma((2, 8)),
            dma((2, 8)),
            dma((4,)),
        ],
        compiler_params=pltpu.CompilerParams(
            collective_id=0, has_side_effects=True, vmem_limit_bytes=58 * 1024 * 1024
        ),
        name="step",
    )(
        queries[0, 0], keys[0, 0], values[0, 0], residual[0, 0], w_out[0],
        event_ids, lengths.reshape(1, 128), type_weight.reshape(1, 1024), gain,
    )
    loss, dq, dk, dv, dwo = pl.pallas_call(
        finish,
        out_shape=(
            jax.ShapeDtypeStruct((1, 1), F32), big, big, big, jax.ShapeDtypeStruct((BLK, D), F32)
        ),
        in_specs=[vmem] * 5,
        out_specs=(vmem, hbm, hbm, hbm, hbm),
        scratch_shapes=[pltpu.VMEM((BLK, D), F32), dma((4,))],
        compiler_params=pltpu.CompilerParams(vmem_limit_bytes=4 * 1024 * 1024),
        name="finish",
    )(loss, dq, dk, dv, dwo)
    return loss, dq[None, None], dk[None, None], dv[None, None], dwo[None]


def solution(mesh):
    hist = P("copy", ("dp", "fsdp"), None, None)
    return jax.shard_map(
        body,
        mesh=mesh,
        in_specs=(
            hist, hist, hist, hist, P(("dp", "fsdp"), None), P(), P(),
            P("copy", "fsdp", None), P("copy", None),
        ),
        out_specs=(
            P("copy", ("dp", "fsdp")), hist, hist, hist, P("copy", "fsdp", None),
        ),
        check_vma=False,
    )
```
